256 devices in a mesh: gx: 4 (over x), gy: 8 (over z_hi, core), gz: 8 (over z_lo, y).
Axes of the slice: x: 4, y: 4, z: 8 (z_hi: 4, z_lo: 2; z = z_hi * 2 + z_lo), core: 2. Of those that a mesh axis runs over, the one named last changes fastest.
Arguments:
- amplitudes: bfloat16 [131072, 4096], P(('gx', 'gy', 'gz')), may hold values from -6 to 6
- tile_coords: int32 [131072, 2], P(('gx', 'gy', 'gz')), may hold values from 0 to 3149, as said below
- row_slot: int32 [3150], replicated, may hold values from 0 to 3321, as said below
- kc_slot: int32 [3150], replicated, may hold values from 0 to 3192, as said below
- integrals: bfloat16 [3200, 64, 256], P(('gy', 'gz')), may hold values from -0.125 to 0.125
Outputs:
- cycle: bfloat16 [3328, 64, 256], P(('gx', 'gy', 'gz'))
The draws below stay inside these ranges and needn't reach their ends.
Inputs may be any that keep to these rules, and one draw needn't show every extreme that they name: `tile_coords`: column 0 is a row tile i * 21 + A, column 1 a contraction tile k * 21 + C. A tile's compute device is the device whose gx times the devices along gy plus gy equals row_slot[column 0] // 104, and whose gz equals (kc_slot[column 1] // 50) modulo the devices along gz. At most 4 tiles of one device's list share a compute device; for 32 compute devices every device's list holds exactly 4. `row_slot`: distinct values. Row tiles are dealt to the groups in turn, so the groups' counts differ by at most one, and the row tiles of group g fill the slots from g * 104 upward without gaps. `kc_slot`: distinct values. Contraction tiles are dealt to the groups along gz in turn; the m-th tile of a group has slot (m // 50) * 50 * (devices along gz) + group * 50 + m % 50.
All inputs are finite; a program needn't handle non-finite values.
Results may differ from the reference program's by a relative error of at most 0.013.
Values may be sent and summed in bfloat16 or wider, within the bound.
No kernel may reach another device: no remote copies, remote signals or barrier semaphores. Data moves between devices by JAX's collectives and lax.ppermute only.
A program may use at most 192 MiB of HBM per device.

```python
import math
import jax
import jax.numpy as jnp
from jax import lax

TILE = 64
TILES_DEV = 512
NRT = 3150
NKT = 3150
JB = 256
NNZ = 131072
CAPD = 4
HEAVY = 32
RSLOTS = 104
KPIECE = 50
N_GX = 4
N_GY = 8
N_GZ = 8
DEVICES = 256


def deal_slots(key):
    groups = N_GX * N_GY
    row_perm = jax.random.permutation(jax.random.fold_in(key, 101), NRT).astype(jnp.int32)
    dealt = jnp.arange(NRT, dtype=jnp.int32)
    row_place = dealt % groups * RSLOTS + dealt // groups
    row_slot = jnp.zeros((NRT,), jnp.int32).at[row_perm].set(row_place)
    kc_perm = jax.random.permutation(jax.random.fold_in(key, 102), NKT).astype(jnp.int32)
    kc_dealt = jnp.arange(NKT, dtype=jnp.int32)
    in_group = kc_dealt // N_GZ
    kc_place = in_group // KPIECE * (N_GZ * KPIECE) + kc_dealt % N_GZ * KPIECE + in_group % KPIECE
    kc_slot = jnp.zeros((NKT,), jnp.int32).at[kc_perm].set(kc_place)
    return (row_perm, row_slot, kc_perm, kc_slot)


def draw_row_slot(key, part):
    return deal_slots(key)[1]


def draw_kc_slot(key, part):
    return deal_slots(key)[3]


def draw_tile_coords(key, part):
    row_perm, row_slot, kc_perm, kc_slot = deal_slots(key)
    groups = N_GX * N_GY
    item_count = DEVICES * CAPD
    heavy_order = jax.random.permutation(jax.random.fold_in(key, 103), DEVICES).astype(jnp.int32)
    heavy_flag = jnp.zeros((DEVICES,), jnp.int32).at[heavy_order[:HEAVY]].set(1)
    item_ids = jnp.arange(item_count, dtype=jnp.int32)
    jitter = jax.random.randint(jax.random.fold_in(key, 104), (DEVICES, item_count), 0, 4096, dtype=jnp.int32)
    scores = (jnp.take(heavy_flag, item_ids // CAPD)[None, :] * 4096 + jitter) * 65536 + item_ids[None, :]
    top_scores, chosen = lax.top_k(scores, TILES_DEV)
    mixing = jax.random.randint(jax.random.fold_in(key, 105), (DEVICES, TILES_DEV), 0, 4096, dtype=jnp.int32)
    mixing = mixing * TILES_DEV + jnp.arange(TILES_DEV, dtype=jnp.int32)[None, :]
    shuffle = jnp.argsort(mixing, axis=1, stable=True).astype(jnp.int32)
    chosen = jnp.take_along_axis(chosen.astype(jnp.int32), shuffle, axis=1)
    target = chosen // CAPD
    row_group = target // N_GZ
    kc_group = target % N_GZ
    row_count = (NRT - row_group + groups - 1) // groups
    pick_row = jax.random.randint(jax.random.fold_in(key, 106), (DEVICES, TILES_DEV), 0, 1 << 20, dtype=jnp.int32) % row_count
    row_tile = jnp.take(row_perm, pick_row * groups + row_group)
    kc_count = (NKT - kc_group + N_GZ - 1) // N_GZ
    pick_kc = jax.random.randint(jax.random.fold_in(key, 107), (DEVICES, TILES_DEV), 0, 1 << 20, dtype=jnp.int32) % kc_count
    kc_tile = jnp.take(kc_perm, pick_kc * N_GZ + kc_group)
    return jnp.stack([row_tile, kc_tile], axis=-1).reshape(NNZ, 2).astype(jnp.int32)


def level_of(key, shape, cuts, smallest, largest):
    factor_of, own = 1.0, jax.random.fold_in(key, 6)
    for position, shards_of in cuts:
        heights = jnp.exp(jax.random.uniform(jax.random.fold_in(own, position), (shards_of,), jnp.float32, smallest / len(cuts), largest / len(cuts)))
        factor_of = factor_of * jnp.repeat(heights, shape[position] // shards_of).reshape([-1 if axis == position else 1 for axis in range(len(shape))])
    return factor_of


def noise(rng, shape, scale, bound, split=(), kind=jnp.bfloat16):
    result = jax.random.normal(rng, shape, jnp.float32) * scale
    if len(split) > 0:
        result = level_of(rng, shape, split, -0.22, 0.18) * result
    return jnp.clip(result, min=-bound, max=bound).astype(kind)


def setup_inputs(seed: int = 0) -> dict:
    key_list = jax.random.split(jax.random.key(seed), 6)
    amplitudes = noise(key_list[0], (NNZ, TILE * TILE), 1.0, 6.0, ((0, 256),))
    tile_coords = draw_tile_coords(jax.random.fold_in(key_list[5], 71), 0)
    row_slot = draw_row_slot(jax.random.fold_in(key_list[5], 71), 0)
    kc_slot = draw_kc_slot(jax.random.fold_in(key_list[5], 71), 0)
    integrals = noise(key_list[4], (N_GY * N_GZ * KPIECE, TILE, JB), (TILE * NNZ // NRT) ** -0.5, 0.125, ((0, 64),))
    return {"amplitudes": amplitudes, "tile_coords": tile_coords, "row_slot": row_slot, "kc_slot": kc_slot, "integrals": integrals}


def reference(amplitudes, tile_coords, row_slot, kc_slot, integrals):
    block_rows = math.gcd(NNZ, 1024)
    n_blocks = NNZ // block_rows
    slot_total = N_GX * N_GY * RSLOTS
    row_pos = jnp.take(row_slot, tile_coords[:, 0].astype(jnp.int32)).astype(jnp.int32)
    kc_pos = jnp.take(kc_slot, tile_coords[:, 1].astype(jnp.int32)).astype(jnp.int32)
    group_of = ((kc_pos // KPIECE) % N_GZ).astype(jnp.int32)
    blocks = amplitudes.reshape(n_blocks, block_rows, TILE, TILE)
    kc_blocks = kc_pos.reshape(n_blocks, block_rows)
    total = jnp.zeros((slot_total, TILE, JB), jnp.float32)
    for group in range(N_GZ):
        masked_rows = jnp.where(group_of == group, row_pos, slot_total).astype(jnp.int32)

        def add_block(running, pieces):
            part_tiles, part_rows, part_kc = pieces
            chosen = jnp.take(integrals, part_kc, axis=0)
            product = jnp.einsum("nac,ncj->naj", part_tiles.astype(jnp.float32), chosen.astype(jnp.float32))
            return running.at[part_rows].add(product, mode="drop"), None

        partial_value = jnp.zeros((slot_total, TILE, JB), jnp.float32)
        partial_value, _ = lax.scan(add_block, partial_value, (blocks, masked_rows.reshape(n_blocks, block_rows), kc_blocks))
        rounded = lax.optimization_barrier(partial_value.astype(jnp.bfloat16))
        total = total + rounded.astype(jnp.float32)
    return total.astype(jnp.bfloat16)
```

```python
import functools

import jax
import jax.numpy as jnp
from jax import lax
from jax.experimental import pallas as pl
from jax.experimental.pallas import tpu as pltpu
from jax.sharding import Mesh, PartitionSpec as P

ALL = ("gx", "zhi", "core", "gz")
GY = ("zhi", "core")
CAP = 4
CHUNKS = (3, 1)
VMEM_LIMIT = 62 * 1024 * 1024


def _relayout_kernel(src_ref, x_ref, out_ref, y_ref, tmp):
    tiles = x_ref.shape[0]
    q_rows = x_ref.shape[1] // 128
    span = 8 * q_rows

    @pl.when(pl.program_id(0) == 0)
    def _():
        def one(g, carry):
            v = x_ref[pl.ds(pl.multiple_of(g * 8, 8), 8), :].astype(jnp.float32)
            for q in range(q_rows):
                tmp[pl.ds(q, 8, stride=q_rows), :] = v[:, q * 128:(q + 1) * 128]
            y_ref[pl.ds(pl.multiple_of(g * span, span), span), :] = tmp[...].astype(y_ref.dtype)
            return carry

        lax.fori_loop(0, tiles // 8, one, 0, unroll=2)

    _copy_slots(src_ref, y_ref, out_ref, q_rows)


def _copy_slots(src_ref, y_ref, out_ref, q_rows):
    slots = out_ref.shape[0] // q_rows
    base = pl.program_id(0) * slots

    def one(s, carry):
        n = src_ref[base + s]
        out_ref[pl.ds(pl.multiple_of(s * q_rows, q_rows), q_rows), :] = y_ref[
            pl.ds(pl.multiple_of(n * q_rows, q_rows), q_rows), :
        ]
        return carry

    lax.fori_loop(0, slots, one, 0, unroll=16)


def _copy_kernel(src_ref, y_ref, held_ref, out_ref, kept_ref):
    _copy_slots(src_ref, y_ref, out_ref, 32)


def first_send(src, x, block):
    tiles, width = x.shape
    q_rows = width // 128
    slots = src.shape[0]
    return pl.pallas_call(
        _relayout_kernel,
        grid_spec=pltpu.PrefetchScalarGridSpec(
            num_scalar_prefetch=1,
            grid=(slots // block,),
            in_specs=[pl.BlockSpec((tiles, width), lambda i, s: (0, 0))],
            out_specs=[
                pl.BlockSpec((block * q_rows, 128), lambda i, s: (i, 0)),
                pl.BlockSpec((tiles * q_rows, 128), lambda i, s: (0, 0)),
            ],
            scratch_shapes=[pltpu.VMEM((8 * q_rows, 128), jnp.float32)],
        ),
        out_shape=[
            jax.ShapeDtypeStruct((slots * q_rows, 128), x.dtype),
            jax.ShapeDtypeStruct((tiles * q_rows, 128), x.dtype),
        ],
        compiler_params=pltpu.CompilerParams(vmem_limit_bytes=VMEM_LIMIT),
        name="first_send",
    )(src, x)


def next_send(src, y, held, block):
    rows = y.shape[0]
    slots = src.shape[0]
    return pl.pallas_call(
        _copy_kernel,
        grid_spec=pltpu.PrefetchScalarGridSpec(
            num_scalar_prefetch=1,
            grid=(slots // block,),
            in_specs=[
                pl.BlockSpec((rows, 128), lambda i, s: (0, 0)),
                pl.BlockSpec(memory_space=pl.ANY),
            ],
            out_specs=[
                pl.BlockSpec((block * 32, 128), lambda i, s: (i, 0)),
                pl.BlockSpec(memory_space=pl.ANY),
            ],
        ),
        out_shape=[
            jax.ShapeDtypeStruct((slots * 32, 128), y.dtype),
            jax.ShapeDtypeStruct(held.shape, held.dtype),
        ],
        input_output_aliases={2: 1},
        compiler_params=pltpu.CompilerParams(vmem_limit_bytes=VMEM_LIMIT),
        name="next_send",
    )(src, y, held)


def _product_kernel(has_in, last, unroll, place_ref, x_ref, w_hbm, *rest):
    if has_in:
        acc_in, out_ref, acc, wbuf, prod, sem = rest
    else:
        out_ref, acc, wbuf, prod, sem = rest
    step = pl.program_id(0)
    edge = 64
    out_rows = out_ref.shape[0]

    @pl.when(step == 0)
    def _():
        copy = pltpu.make_async_copy(w_hbm, wbuf, sem.at[0])
        copy.start()
        if has_in:
            back = pltpu.make_async_copy(acc_in, acc.at[pl.ds(0, out_rows), :], sem.at[1])
            back.start()
            back.wait()
        else:
            acc[...] = jnp.zeros_like(acc)
        copy.wait()

    block = x_ref.shape[0] // 32
    base = step * block

    def group(i, carry):
        rows = []
        for u in range(unroll):
            n = i * unroll + u
            v = place_ref[base + n]
            row = lax.shift_right_logical(v, 10)
            kc = lax.bitwise_and(v, 1023)
            rows.append(row)
            p = x_ref[pl.ds(pl.multiple_of(n * 32, 32), 32), :]
            a = jnp.concatenate([p[:, :64], p[:, 64:]], axis=0)
            w = jnp.concatenate(
                [wbuf[pl.ds(pl.multiple_of((kc + 400 * k) * 16, 16), 16), :] for k in range(4)], axis=0
            )
            prod[u] = jnp.dot(a, w, preferred_element_type=jnp.float32)
        for u in range(unroll):
            where = pl.ds(pl.multiple_of(rows[u] * edge, edge), edge)
            acc[where, :] += prod[u]
        return carry

    lax.fori_loop(0, block // unroll, group, 0)

    @pl.when(step == pl.num_programs(0) - 1)
    def _():
        if last:
            out_ref[...] = acc[pl.ds(0, out_rows), :].astype(out_ref.dtype)
        else:
            away = pltpu.make_async_copy(acc.at[pl.ds(0, out_rows), :], out_ref, sem.at[1])
            away.start()
            away.wait()


def products(place, x, w, acc_in, row_local, last, block=64, unroll=8):
    tiles = place.shape[0]
    has_in = acc_in is not None
    rows = row_local * 64
    operands = (place, x, w) + ((acc_in,) if has_in else ())
    return pl.pallas_call(
        functools.partial(_product_kernel, has_in, last, unroll),
        grid_spec=pltpu.PrefetchScalarGridSpec(
            num_scalar_prefetch=1,
            grid=(tiles // block,),
            in_specs=[
                pl.BlockSpec((block * 32, 128), lambda i, s: (i, 0)),
                pl.BlockSpec(memory_space=pl.ANY),
            ] + ([pl.BlockSpec(memory_space=pl.ANY)] if has_in else []),
            out_specs=pl.BlockSpec((rows, 256), lambda i, s: (0, 0)) if last
            else pl.BlockSpec(memory_space=pl.ANY),
            scratch_shapes=[
                pltpu.VMEM((rows + 64, 256), jnp.float32),
                pltpu.VMEM(w.shape, w.dtype),
                pltpu.VMEM((unroll, 64, 256), jnp.float32),
                pltpu.SemaphoreType.DMA((2,)),
            ],
        ),
        out_shape=jax.ShapeDtypeStruct((rows, 256), jnp.bfloat16 if last else jnp.float32),
        compiler_params=pltpu.CompilerParams(vmem_limit_bytes=VMEM_LIMIT),
        name="products",
    )(*operands)


def body(amplitudes, tile_coords, row_slot, kc_slot, integrals):
    kc_groups = lax.axis_size("gz")
    planes = lax.axis_size("gx")
    devices = planes * lax.axis_size("zhi") * lax.axis_size("core") * kc_groups
    tile_count = amplitudes.shape[0]
    kc_piece, tile_edge, columns = integrals.shape
    row_local = 104
    gy_size = lax.axis_size("zhi") * lax.axis_size("core")
    part = tile_edge // planes
    quarter = lax.dynamic_slice_in_dim(integrals, lax.axis_index("gx") * part, part, 1)
    quarter = quarter.reshape(kc_piece * part, columns)
    slab = lax.all_gather(quarter, "zhi", axis=0, tiled=True)

    row_pos = jnp.take(row_slot, tile_coords[:, 0])
    kc_pos = jnp.take(kc_slot, tile_coords[:, 1])
    kc_target = kc_pos // kc_piece % kc_groups
    kc_gy = kc_pos // (kc_groups * kc_piece)
    kc_row = kc_gy % 2 * (kc_piece * gy_size // 2) + kc_gy // 2 * kc_piece + kc_pos % kc_piece
    place = row_pos % row_local * 1024 + kc_row
    target = row_pos // row_local * kc_groups + kc_target
    ids = jnp.arange(tile_count, dtype=jnp.int32)
    same = (target[:, None] == target[None, :]) & (ids[None, :] < ids[:, None])
    rank = jnp.sum(same.astype(jnp.int32), axis=1)
    send_index = rank * devices + target
    send_ids = jnp.arange(devices * CAP, dtype=jnp.int32)
    matches = send_ids[:, None] == send_index[None, :]
    source = jnp.sum(jnp.where(matches, ids[None, :], 0), axis=1)
    empty = row_local * 1024
    sent_place = empty + jnp.sum(jnp.where(matches, place[None, :] - empty, 0), axis=1)
    source = source.reshape(CAP, devices)
    sent_place = sent_place.reshape(CAP, devices).T
    got_place = lax.all_to_all(sent_place, ALL, split_axis=0, concat_axis=0, tiled=True)

    acc = None
    start = 0
    relaid = None
    got = []
    for size in CHUNKS:
        src = source[start:start + size].T.reshape(-1)
        if relaid is None:
            sent, relaid = first_send(src, amplitudes, 64)
        else:
            sent, slab = next_send(src, relaid, slab, 64)
            slab = lax.all_gather(slab, ("gx", "core"), axis=0, tiled=True)
        arrived = lax.all_to_all(
            sent.reshape(devices, size * 32, 128), ALL, split_axis=0, concat_axis=0, tiled=True
        )
        got.append((arrived.reshape(devices * size * 32, 128), got_place[:, start:start + size].reshape(-1)))
        start += size
    for index, (tiles, places) in enumerate(got):
        acc = products(places, tiles, slab, acc, row_local, index == len(got) - 1)
    shared = lax.all_to_all(
        acc.reshape(kc_groups, row_local // kc_groups * tile_edge, columns), "gz", split_axis=0, concat_axis=0, tiled=True
    )
    total = jnp.sum(shared.astype(jnp.float32), axis=0).astype(jnp.bfloat16)
    total = total.reshape(row_local // kc_groups, 2, tile_edge // 2, columns)
    return jnp.swapaxes(total, 1, 2).reshape(row_local // kc_groups, tile_edge, columns)


def solution(mesh):
    gx, gy, gz = mesh.devices.shape
    fine = Mesh(mesh.devices.reshape(gx, gy // 2, 2, gz), ALL)
    placed = (
        P(ALL, None),
        P(ALL, None),
        P(),
        P(),
        P(GY + ("gz",), None, None),
    )

    return jax.shard_map(
        body, mesh=fine, in_specs=placed, out_specs=P(ALL, None, None), check_vma=False
    )
```

```python
import functools

import jax
import jax.numpy as jnp
from jax import lax
from jax.experimental import pallas as pl
from jax.experimental.pallas import tpu as pltpu
from jax.sharding import Mesh, PartitionSpec as P

ALL = ("gx", "zhi", "core", "gz")
GY = ("zhi", "core")
CAP = 4
CHUNKS = (3, 1)
VMEM_LIMIT = 62 * 1024 * 1024


def _relayout_kernel(src_ref, x_ref, out_ref, y_ref, tmp):
    tiles = x_ref.shape[0]
    q_rows = x_ref.shape[1] // 128
    span = 8 * q_rows

    @pl.when(pl.program_id(0) == 0)
    def _():
        def one(g, carry):
            v = x_ref[pl.ds(pl.multiple_of(g * 8, 8), 8), :].astype(jnp.float32)
            half = lax.rem(g, 2)
            for q in range(q_rows):
                tmp[half, pl.ds(q * 8, 8), :] = v[:, q * 128:(q + 1) * 128]
            for r in range(8):
                y_ref[pl.ds(pl.multiple_of(g * span, span) + r * q_rows, q_rows), :] = tmp[
                    half, pl.ds(r, q_rows, stride=8), :
                ].astype(y_ref.dtype)
            return carry

        lax.fori_loop(0, tiles // 8, one, 0, unroll=2)

    _copy_slots(src_ref, y_ref, out_ref, q_rows)


def _copy_slots(src_ref, y_ref, out_ref, q_rows):
    slots = out_ref.shape[0] // q_rows
    base = pl.program_id(0) * slots

    def one(s, carry):
        n = src_ref[base + s]
        out_ref[pl.ds(pl.multiple_of(s * q_rows, q_rows), q_rows), :] = y_ref[
            pl.ds(pl.multiple_of(n * q_rows, q_rows), q_rows), :
        ]
        return carry

    lax.fori_loop(0, slots, one, 0, unroll=16)


def _copy_kernel(src_ref, y_ref, held_ref, out_ref, kept_ref):
    _copy_slots(src_ref, y_ref, out_ref, 32)


def first_send(src, x, block):
    tiles, width = x.shape
    q_rows = width // 128
    slots = src.shape[0]
    return pl.pallas_call(
        _relayout_kernel,
        grid_spec=pltpu.PrefetchScalarGridSpec(
            num_scalar_prefetch=1,
            grid=(slots // block,),
            in_specs=[pl.BlockSpec((tiles, width), lambda i, s: (0, 0))],
            out_specs=[
                pl.BlockSpec((block * q_rows, 128), lambda i, s: (i, 0)),
                pl.BlockSpec((tiles * q_rows, 128), lambda i, s: (0, 0)),
            ],
            scratch_shapes=[pltpu.VMEM((2, 8 * q_rows, 128), jnp.float32)],
        ),
        out_shape=[
            jax.ShapeDtypeStruct((slots * q_rows, 128), x.dtype),
            jax.ShapeDtypeStruct((tiles * q_rows, 128), x.dtype),
        ],
        compiler_params=pltpu.CompilerParams(vmem_limit_bytes=VMEM_LIMIT),
        name="first_send",
    )(src, x)


def next_send(src, y, held, block):
    rows = y.shape[0]
    slots = src.shape[0]
    return pl.pallas_call(
        _copy_kernel,
        grid_spec=pltpu.PrefetchScalarGridSpec(
            num_scalar_prefetch=1,
            grid=(slots // block,),
            in_specs=[
                pl.BlockSpec((rows, 128), lambda i, s: (0, 0)),
                pl.BlockSpec(memory_space=pl.ANY),
            ],
            out_specs=[
                pl.BlockSpec((block * 32, 128), lambda i, s: (i, 0)),
                pl.BlockSpec(memory_space=pl.ANY),
            ],
        ),
        out_shape=[
            jax.ShapeDtypeStruct((slots * 32, 128), y.dtype),
            jax.ShapeDtypeStruct(held.shape, held.dtype),
        ],
        input_output_aliases={2: 1},
        compiler_params=pltpu.CompilerParams(vmem_limit_bytes=VMEM_LIMIT),
        name="next_send",
    )(src, y, held)


def _product_kernel(has_in, last, block, unroll, place_ref, x_hbm, w_hbm, *rest):
    if has_in:
        acc_in, out_hbm, acc, w_ref, prod, xbuf, before, held, x_sem, sem = rest
    else:
        out_hbm, acc, w_ref, prod, xbuf, x_sem, sem = rest
    rows = out_hbm.shape[0]
    blocks = x_hbm.shape[0] // block

    def fetch(b, slot):
        return pltpu.make_async_copy(x_hbm.at[pl.ds(b * block, block)], xbuf.at[slot], x_sem.at[slot])

    slab = pltpu.make_async_copy(w_hbm, w_ref, sem.at[0])
    slab.start()
    fetch(0, 0).start()
    if has_in:
        back = pltpu.make_async_copy(acc_in, before, sem.at[1])
        back.start()
    acc[...] = jnp.zeros_like(acc)
    slab.wait()

    def one_block(b, carry):
        slot = lax.rem(b, 2)

        @pl.when(b + 1 < blocks)
        def _():
            fetch(b + 1, 1 - slot).start()

        fetch(b, slot).wait()

        def group(i, carry):
            where = []
            for u in range(unroll):
                n = i * unroll + u
                v = place_ref[b * block + n]
                where.append(lax.shift_right_logical(v, 10))
                kc = lax.bitwise_and(v, 1023)
                p = xbuf[slot, n]
                a = jnp.concatenate([p[:, :64], p[:, 64:]], axis=0)
                w = jnp.concatenate([w_ref[k, kc] for k in range(4)], axis=0)
                prod[u] = jnp.dot(a, w, preferred_element_type=jnp.float32)
            for u in range(unroll):
                acc[where[u]] += prod[u]
            return carry

        lax.fori_loop(0, block // unroll, group, 0)
        return carry

    lax.fori_loop(0, blocks, one_block, 0)
    if has_in:
        back.wait()
    if last:
        def finish(r, carry):
            held[r] = (acc[r] + before[r]).astype(held.dtype) if has_in else acc[r].astype(held.dtype)
            return carry

        lax.fori_loop(0, rows, finish, 0, unroll=4)
        away = pltpu.make_async_copy(held, out_hbm, sem.at[2])
    else:
        away = pltpu.make_async_copy(acc.at[pl.ds(0, rows)], out_hbm, sem.at[2])
    away.start()
    away.wait()


def products(place, x, w, acc_in, row_local, last, block=128, unroll=8):
    has_in = acc_in is not None
    operands = (place, x, w) + ((acc_in,) if has_in else ())
    edge, columns = 64, w.shape[-1]
    result = jax.ShapeDtypeStruct((row_local, edge, columns), jnp.bfloat16 if last else jnp.float32)
    return pl.pallas_call(
        functools.partial(_product_kernel, has_in, last, block, unroll),
        in_specs=[pl.BlockSpec(memory_space=pltpu.SMEM)] + [pl.BlockSpec(memory_space=pl.ANY)] * (len(operands) - 1),
        out_specs=pl.BlockSpec(memory_space=pl.ANY),
        scratch_shapes=[
            pltpu.VMEM((row_local + 1, edge, columns), jnp.float32),
            pltpu.VMEM(w.shape, w.dtype),
            pltpu.VMEM((unroll, edge, columns), jnp.float32),
            pltpu.VMEM((2, block, 32, 128), x.dtype),
        ] + ([
            pltpu.VMEM((row_local, edge, columns), jnp.float32),
            pltpu.VMEM(result.shape, result.dtype),
        ] if has_in else []) + [
            pltpu.SemaphoreType.DMA((2,)),
            pltpu.SemaphoreType.DMA((3,)),
        ],
        out_shape=result,
        compiler_params=pltpu.CompilerParams(vmem_limit_bytes=VMEM_LIMIT),
        name="products",
    )(*operands)


def look_up(coords, row_slot, kc_slot):
    count = row_slot.shape[0]
    lines = -(-count // 128)
    tables = jnp.pad(jnp.stack([row_slot, kc_slot]), ((0, 0), (0, lines * 128 - count)))
    tables = tables.reshape(2, lines, 128).astype(jnp.float32)
    line = (coords[:, :, None] // 128 == jnp.arange(lines)).astype(jnp.float32)
    picked = jnp.einsum(
        "tnh,thl->tnl", line, tables, precision=lax.Precision.HIGHEST, preferred_element_type=jnp.float32
    )
    lane = coords[:, :, None] % 128 == jnp.arange(128)
    found = jnp.sum(jnp.where(lane, picked, 0.0), axis=2).astype(jnp.int32)
    return found[0], found[1]


def body(amplitudes, tile_coords, row_slot, kc_slot, integrals):
    kc_groups = lax.axis_size("gz")
    planes = lax.axis_size("gx")
    devices = planes * lax.axis_size("zhi") * lax.axis_size("core") * kc_groups
    tile_count = amplitudes.shape[0]
    kc_piece, tile_edge, columns = integrals.shape
    row_local = 104
    gy_size = lax.axis_size("zhi") * lax.axis_size("core")
    part = tile_edge // planes
    quarter = lax.dynamic_slice_in_dim(integrals, lax.axis_index("gx") * part, part, 1)
    quarter = quarter.reshape(kc_piece * part, columns)
    slab = lax.all_gather(quarter, "zhi", axis=0, tiled=True)

    row_pos, kc_pos = look_up(tile_coords.T, row_slot, kc_slot)
    kc_target = kc_pos // kc_piece % kc_groups
    kc_gy = kc_pos // (kc_groups * kc_piece)
    kc_row = kc_gy % 2 * (kc_piece * gy_size // 2) + kc_gy // 2 * kc_piece + kc_pos % kc_piece
    place = row_pos % row_local * 1024 + kc_row
    target = row_pos // row_local * kc_groups + kc_target
    ids = jnp.arange(tile_count, dtype=jnp.int32)
    same = (target[:, None] == target[None, :]) & (ids[None, :] < ids[:, None])
    rank = jnp.sum(same.astype(jnp.int32), axis=1)
    send_index = rank * devices + target
    send_ids = jnp.arange(devices * CAP, dtype=jnp.int32)
    matches = send_ids[:, None] == send_index[None, :]
    source = jnp.sum(jnp.where(matches, ids[None, :], 0), axis=1)
    empty = row_local * 1024
    sent_place = empty + jnp.sum(jnp.where(matches, place[None, :] - empty, 0), axis=1)
    source = source.reshape(CAP, devices)
    sent_place = sent_place.reshape(CAP, devices).T
    got_place = lax.all_to_all(sent_place, ALL, split_axis=0, concat_axis=0, tiled=True)

    acc = None
    start = 0
    relaid = None
    got = []
    for size in CHUNKS:
        src = source[start:start + size].T.reshape(-1)
        if relaid is None:
            sent, relaid = first_send(src, amplitudes, 64)
        else:
            sent, slab = next_send(src, relaid, slab, 64)
            slab = lax.all_gather(slab, ("gx", "core"), axis=0, tiled=True)
        arrived = lax.all_to_all(sent.reshape(devices, size * 32, 128), ALL, split_axis=0, concat_axis=0, tiled=True)
        got.append((arrived.reshape(devices * size, 32, 128), got_place[:, start:start + size].reshape(-1)))
        start += size
    for index, (tiles, places) in enumerate(got):
        acc = products(places, tiles, slab.reshape(planes, -1, part, columns), acc, row_local, index == len(got) - 1)
    shared = lax.all_to_all(
        acc.reshape(kc_groups, row_local // kc_groups * tile_edge, columns), "gz", split_axis=0, concat_axis=0, tiled=True
    )
    total = jnp.sum(shared.astype(jnp.float32), axis=0).astype(jnp.bfloat16)
    total = total.reshape(row_local // kc_groups, 2, tile_edge // 2, columns)
    return jnp.swapaxes(total, 1, 2).reshape(row_local // kc_groups, tile_edge, columns)


def solution(mesh):
    gx, gy, gz = mesh.devices.shape
    fine = Mesh(mesh.devices.reshape(gx, gy // 2, 2, gz), ALL)
    placed = (
        P(ALL, None),
        P(ALL, None),
        P(),
        P(),
        P(GY + ("gz",), None, None),
    )

    return jax.shard_map(body, mesh=fine, in_specs=placed, out_specs=P(ALL, None, None), check_vma=False)
```

```python
import functools

import jax
import jax.numpy as jnp
from jax import lax
from jax.experimental import pallas as pl
from jax.experimental.pallas import tpu as pltpu
from jax.sharding import Mesh, PartitionSpec as P

ALL = ("gx", "zhi", "core", "gz")
GY = ("zhi", "core")
CAP = 4
RELAYOUT = 4
CHUNKS = (3, 1)
VMEM_LIMIT = 62 * 1024 * 1024


def _relayout_kernel(src_ref, x_ref, out_ref, y_ref, *tmps):
    tiles = x_ref.shape[0]
    q_rows = x_ref.shape[1] // 128
    group = 8 * len(tmps)

    @pl.when(pl.program_id(0) == 0)
    def _():
        def one(g, carry):
            for t, tmp in enumerate(tmps):
                v = x_ref[pl.ds(pl.multiple_of(g * group, group) + 8 * t, 8), :].astype(jnp.float32)
                for q in range(q_rows):
                    tmp[pl.ds(q * 8, 8), :] = v[:, q * 128:(q + 1) * 128]
            for t, tmp in enumerate(tmps):
                for r in range(8):
                    y_ref[g * group + 8 * t + r] = tmp[pl.ds(r, q_rows, stride=8), :].astype(y_ref.dtype)
            return carry

        lax.fori_loop(0, tiles // group, one, 0)

    _copy_slots(src_ref, y_ref, out_ref)


def _copy_slots(src_ref, y_ref, out_ref):
    slots = out_ref.shape[0]
    base = pl.program_id(0) * slots

    def one(g, carry):
        for u in range(16):
            s = g * 16 + u
            out_ref[s] = y_ref[src_ref[base + s]]
        return carry

    lax.fori_loop(0, slots // 16, one, 0)


def _copy_kernel(src_ref, y_ref, held_ref, out_ref, kept_ref):
    _copy_slots(src_ref, y_ref, out_ref)


def first_send(src, x, block):
    tiles, width = x.shape
    q_rows = width // 128
    slots = src.shape[0]
    return pl.pallas_call(
        _relayout_kernel,
        grid_spec=pltpu.PrefetchScalarGridSpec(
            num_scalar_prefetch=1,
            grid=(slots // block,),
            in_specs=[pl.BlockSpec((tiles, width), lambda i, s: (0, 0))],
            out_specs=[
                pl.BlockSpec((block, q_rows, 128), lambda i, s: (i, 0, 0)),
                pl.BlockSpec((tiles, q_rows, 128), lambda i, s: (0, 0, 0)),
            ],
            scratch_shapes=[pltpu.VMEM((8 * q_rows, 128), jnp.float32) for _ in range(RELAYOUT)],
        ),
        out_shape=[
            jax.ShapeDtypeStruct((slots, q_rows, 128), x.dtype),
            jax.ShapeDtypeStruct((tiles, q_rows, 128), x.dtype),
        ],
        compiler_params=pltpu.CompilerParams(vmem_limit_bytes=VMEM_LIMIT),
        name="first_send",
    )(src, x)


def next_send(src, y, held, block):
    slots = src.shape[0]
    return pl.pallas_call(
        _copy_kernel,
        grid_spec=pltpu.PrefetchScalarGridSpec(
            num_scalar_prefetch=1,
            grid=(slots // block,),
            in_specs=[
                pl.BlockSpec(y.shape, lambda i, s: (0, 0, 0)),
                pl.BlockSpec(memory_space=pl.ANY),
            ],
            out_specs=[
                pl.BlockSpec((block,) + y.shape[1:], lambda i, s: (i, 0, 0)),
                pl.BlockSpec(memory_space=pl.ANY),
            ],
        ),
        out_shape=[
            jax.ShapeDtypeStruct((slots,) + y.shape[1:], y.dtype),
            jax.ShapeDtypeStruct(held.shape, held.dtype),
        ],
        input_output_aliases={2: 1},
        compiler_params=pltpu.CompilerParams(vmem_limit_bytes=VMEM_LIMIT),
        name="next_send",
    )(src, y, held)


def _product_kernel(has_in, last, block, unroll, place_ref, x_hbm, w_hbm, *rest):
    if has_in:
        acc_in, out_hbm, acc, w_ref, prod, xbuf, before, held, x_sem, sem = rest
    else:
        out_hbm, acc, w_ref, prod, xbuf, x_sem, sem = rest
    rows = out_hbm.shape[0]
    blocks = x_hbm.shape[0] // block

    def fetch(b, slot):
        return pltpu.make_async_copy(x_hbm.at[pl.ds(b * block, block)], xbuf.at[slot], x_sem.at[slot])

    slab = pltpu.make_async_copy(w_hbm, w_ref, sem.at[0])
    slab.start()
    fetch(0, 0).start()
    if has_in:
        back = pltpu.make_async_copy(acc_in, before, sem.at[1])
        back.start()
    acc[...] = jnp.zeros_like(acc)
    slab.wait()

    def one_block(b, carry):
        slot = lax.rem(b, 2)

        @pl.when(b + 1 < blocks)
        def _():
            fetch(b + 1, 1 - slot).start()

        fetch(b, slot).wait()

        def group(i, carry):
            where = []
            for u in range(unroll):
                n = i * unroll + u
                v = place_ref[b * block + n]
                where.append(lax.shift_right_logical(v, 10))
                kc = lax.bitwise_and(v, 1023)
                p = xbuf[slot, n]
                a = jnp.concatenate([p[:, :64], p[:, 64:]], axis=0)
                w = jnp.concatenate([w_ref[k, kc] for k in range(4)], axis=0)
                prod[u] = jnp.dot(a, w, preferred_element_type=jnp.float32)
            for u in range(unroll):
                acc[where[u]] += prod[u]
            return carry

        lax.fori_loop(0, block // unroll, group, 0)
        return carry

    lax.fori_loop(0, blocks, one_block, 0)
    if has_in:
        back.wait()
    if last:
        def finish(r, carry):
            held[r] = (acc[r] + before[r]).astype(held.dtype) if has_in else acc[r].astype(held.dtype)
            return carry

        lax.fori_loop(0, rows, finish, 0, unroll=4)
        away = pltpu.make_async_copy(held, out_hbm, sem.at[2])
    else:
        away = pltpu.make_async_copy(acc.at[pl.ds(0, rows)], out_hbm, sem.at[2])
    away.start()
    away.wait()


def products(place, x, w, acc_in, row_local, last, block=128, unroll=32):
    has_in = acc_in is not None
    operands = (place, x, w) + ((acc_in,) if has_in else ())
    edge, columns = 64, w.shape[-1]
    result = jax.ShapeDtypeStruct((row_local, edge, columns), jnp.bfloat16 if last else jnp.float32)
    return pl.pallas_call(
        functools.partial(_product_kernel, has_in, last, block, unroll),
        in_specs=[pl.BlockSpec(memory_space=pltpu.SMEM)] + [pl.BlockSpec(memory_space=pl.ANY)] * (len(operands) - 1),
        out_specs=pl.BlockSpec(memory_space=pl.ANY),
        scratch_shapes=[
            pltpu.VMEM((row_local + 1, edge, columns), jnp.float32),
            pltpu.VMEM(w.shape, w.dtype),
            pltpu.VMEM((unroll, edge, columns), jnp.float32),
            pltpu.VMEM((2, block, 32, 128), x.dtype),
        ] + ([
            pltpu.VMEM((row_local, edge, columns), jnp.float32),
            pltpu.VMEM(result.shape, result.dtype),
        ] if has_in else []) + [
            pltpu.SemaphoreType.DMA((2,)),
            pltpu.SemaphoreType.DMA((3,)),
        ],
        out_shape=result,
        compiler_params=pltpu.CompilerParams(vmem_limit_bytes=VMEM_LIMIT),
        name="products",
    )(*operands)


def look_up(coords, row_slot, kc_slot):
    count = row_slot.shape[0]
    lines = -(-count // 128)
    tables = jnp.pad(jnp.stack([row_slot, kc_slot]), ((0, 0), (0, lines * 128 - count)))
    tables = tables.reshape(2, lines, 128).astype(jnp.float32)
    line = (coords[:, :, None] // 128 == jnp.arange(lines)).astype(jnp.float32)
    picked = jnp.einsum(
        "tnh,thl->tnl", line, tables, precision=lax.Precision.HIGHEST, preferred_element_type=jnp.float32
    )
    lane = coords[:, :, None] % 128 == jnp.arange(128)
    found = jnp.sum(jnp.where(lane, picked, 0.0), axis=2).astype(jnp.int32)
    return found[0], found[1]


def body(amplitudes, tile_coords, row_slot, kc_slot, integrals):
    kc_groups = lax.axis_size("gz")
    planes = lax.axis_size("gx")
    devices = planes * lax.axis_size("zhi") * lax.axis_size("core") * kc_groups
    tile_count = amplitudes.shape[0]
    kc_piece, tile_edge, columns = integrals.shape
    row_local = 104
    gy_size = lax.axis_size("zhi") * lax.axis_size("core")
    part = tile_edge // planes
    quarter = lax.dynamic_slice_in_dim(integrals, lax.axis_index("gx") * part, part, 1)
    quarter = quarter.reshape(kc_piece * part, columns)
    slab = lax.all_gather(quarter, "zhi", axis=0, tiled=True)

    row_pos, kc_pos = look_up(tile_coords.T, row_slot, kc_slot)
    kc_target = kc_pos // kc_piece % kc_groups
    kc_gy = kc_pos // (kc_groups * kc_piece)
    kc_row = kc_gy % 2 * (kc_piece * gy_size // 2) + kc_gy // 2 * kc_piece + kc_pos % kc_piece
    place = row_pos % row_local * 1024 + kc_row
    target = row_pos // row_local * kc_groups + kc_target
    ids = jnp.arange(tile_count, dtype=jnp.int32)
    same = (target[:, None] == target[None, :]) & (ids[None, :] < ids[:, None])
    rank = jnp.sum(same.astype(jnp.int32), axis=1)
    send_index = rank * devices + target
    send_ids = jnp.arange(devices * CAP, dtype=jnp.int32)
    matches = send_ids[:, None] == send_index[None, :]
    source = jnp.sum(jnp.where(matches, ids[None, :], 0), axis=1)
    empty = row_local * 1024
    sent_place = empty + jnp.sum(jnp.where(matches, place[None, :] - empty, 0), axis=1)
    source = source.reshape(CAP, devices)
    sent_place = sent_place.reshape(CAP, devices).T
    got_place = lax.all_to_all(sent_place, ALL, split_axis=0, concat_axis=0, tiled=True)

    acc = None
    start = 0
    relaid = None
    got = []
    for size in CHUNKS:
        src = source[start:start + size].T.reshape(-1)
        if relaid is None:
            sent, relaid = first_send(src, amplitudes, 64)
        else:
            sent, slab = next_send(src, relaid, slab, 64)
            slab = lax.all_gather(slab, ("gx", "core"), axis=0, tiled=True)
        arrived = lax.all_to_all(sent.reshape(devices, size * 32, 128), ALL, split_axis=0, concat_axis=0, tiled=True)
        got.append((arrived.reshape(devices * size, 32, 128), got_place[:, start:start + size].reshape(-1)))
        start += size
    for index, (tiles, places) in enumerate(got):
        acc = products(places, tiles, slab.reshape(planes, -1, part, columns), acc, row_local, index == len(got) - 1)
    shared = lax.all_to_all(
        acc.reshape(kc_groups, row_local // kc_groups * tile_edge, columns), "gz", split_axis=0, concat_axis=0, tiled=True
    )
    total = jnp.sum(shared.astype(jnp.float32), axis=0).astype(jnp.bfloat16)
    total = total.reshape(row_local // kc_groups, 2, tile_edge // 2, columns)
    return jnp.swapaxes(total, 1, 2).reshape(row_local // kc_groups, tile_edge, columns)


def solution(mesh):
    gx, gy, gz = mesh.devices.shape
    fine = Mesh(mesh.devices.reshape(gx, gy // 2, 2, gz), ALL)
    placed = (
        P(ALL, None),
        P(ALL, None),
        P(),
        P(),
        P(GY + ("gz",), None, None),
    )

    return jax.shard_map(body, mesh=fine, in_specs=placed, out_specs=P(ALL, None, None), check_vma=False)
```

```python
import functools

import jax
import jax.numpy as jnp
from jax import lax
from jax.experimental import pallas as pl
from jax.experimental.pallas import tpu as pltpu
from jax.sharding import Mesh, PartitionSpec as P

ALL = ("gx", "zhi", "core", "gz")
GY = ("zhi", "core")
CAP = 4
RELAYOUT = 4
CHUNKS = (3, 1)
VMEM_LIMIT = 62 * 1024 * 1024


def _relayout_kernel(src_ref, x_ref, out_ref, y_ref, *tmps):
    tiles = x_ref.shape[0]
    q_rows = x_ref.shape[1] // 128
    group = 8 * len(tmps)

    @pl.when(pl.program_id(0) == 0)
    def _():
        def one(g, carry):
            for t, tmp in enumerate(tmps):
                v = x_ref[pl.ds(pl.multiple_of(g * group, group) + 8 * t, 8), :].astype(jnp.float32)
                for q in range(q_rows):
                    tmp[pl.ds(q * 8, 8), :] = v[:, q * 128:(q + 1) * 128]
            for t, tmp in enumerate(tmps):
                for r in range(8):
                    y_ref[g * group + 8 * t + r] = tmp[pl.ds(r, q_rows, stride=8), :].astype(y_ref.dtype)
            return carry

        lax.fori_loop(0, tiles // group, one, 0)

    _copy_slots(src_ref, y_ref, out_ref)


def _copy_slots(src_ref, y_ref, out_ref):
    slots = out_ref.shape[0]
    base = pl.program_id(0) * slots

    def one(g, carry):
        for u in range(16):
            s = g * 16 + u
            out_ref[s] = y_ref[src_ref[base + s]]
        return carry

    lax.fori_loop(0, slots // 16, one, 0)


def _copy_kernel(src_ref, y_ref, held_ref, out_ref, kept_ref):
    _copy_slots(src_ref, y_ref, out_ref)


def first_send(src, x, block):
    tiles, width = x.shape
    q_rows = width // 128
    slots = src.shape[0]
    return pl.pallas_call(
        _relayout_kernel,
        grid_spec=pltpu.PrefetchScalarGridSpec(
            num_scalar_prefetch=1,
            grid=(slots // block,),
            in_specs=[pl.BlockSpec((tiles, width), lambda i, s: (0, 0))],
            out_specs=[
                pl.BlockSpec((block, q_rows, 128), lambda i, s: (i, 0, 0)),
                pl.BlockSpec((tiles, q_rows, 128), lambda i, s: (0, 0, 0)),
            ],
            scratch_shapes=[pltpu.VMEM((8 * q_rows, 128), jnp.float32) for _ in range(RELAYOUT)],
        ),
        out_shape=[
            jax.ShapeDtypeStruct((slots, q_rows, 128), x.dtype),
            jax.ShapeDtypeStruct((tiles, q_rows, 128), x.dtype),
        ],
        compiler_params=pltpu.CompilerParams(vmem_limit_bytes=VMEM_LIMIT),
        name="first_send",
    )(src, x)


def next_send(src, y, held, block):
    slots = src.shape[0]
    return pl.pallas_call(
        _copy_kernel,
        grid_spec=pltpu.PrefetchScalarGridSpec(
            num_scalar_prefetch=1,
            grid=(slots // block,),
            in_specs=[
                pl.BlockSpec(y.shape, lambda i, s: (0, 0, 0)),
                pl.BlockSpec(memory_space=pl.ANY),
            ],
            out_specs=[
                pl.BlockSpec((block,) + y.shape[1:], lambda i, s: (i, 0, 0)),
                pl.BlockSpec(memory_space=pl.ANY),
            ],
        ),
        out_shape=[
            jax.ShapeDtypeStruct((slots,) + y.shape[1:], y.dtype),
            jax.ShapeDtypeStruct(held.shape, held.dtype),
        ],
        input_output_aliases={2: 1},
        compiler_params=pltpu.CompilerParams(vmem_limit_bytes=VMEM_LIMIT),
        name="next_send",
    )(src, y, held)


def _held_kernel(*refs):
    pass


def held_until(values):
    count = len(values)
    return list(pl.pallas_call(
        _held_kernel,
        in_specs=[pl.BlockSpec(memory_space=pl.ANY)] * count,
        out_specs=[pl.BlockSpec(memory_space=pl.ANY)] * count,
        out_shape=[jax.ShapeDtypeStruct(v.shape, v.dtype) for v in values],
        input_output_aliases={i: i for i in range(count)},
        name="held_until",
    )(*values))


def _product_kernel(has_in, last, block, unroll, place_ref, own_ref, x_hbm, *rest):
    parts, rest = rest[:8], rest[8:]
    if has_in:
        acc_in, out_hbm, acc, w_ref, prod, xbuf, before, held, w_sem, x_sem, sem = rest
    else:
        out_hbm, acc, w_ref, prod, xbuf, w_sem, x_sem, sem = rest
    rows = out_hbm.shape[0]
    blocks = x_hbm.shape[0] // block

    def fetch(b, slot):
        return pltpu.make_async_copy(x_hbm.at[pl.ds(b * block, block)], xbuf.at[slot], x_sem.at[slot])

    copies = []
    for index, part in enumerate(parts):
        plane = lax.rem(own_ref[0] + 4 - index % 4, 4)
        core = lax.rem(own_ref[2] + index // 4, 2)
        for back_z in range(4):
            first = (core * 4 + lax.rem(own_ref[1] + 4 - back_z, 4)) * 50
            copies.append(pltpu.make_async_copy(
                part.at[back_z], w_ref.at[plane, pl.ds(first, 50)], w_sem.at[index * 4 + back_z]
            ))
    for copy in copies:
        copy.start()
    fetch(0, 0).start()
    if has_in:
        back = pltpu.make_async_copy(acc_in, before, sem.at[1])
        back.start()
    acc[...] = jnp.zeros_like(acc)
    for copy in copies:
        copy.wait()

    def one_block(b, carry):
        slot = lax.rem(b, 2)

        @pl.when(b + 1 < blocks)
        def _():
            fetch(b + 1, 1 - slot).start()

        fetch(b, slot).wait()

        def group(i, carry):
            where = []
            for u in range(unroll):
                n = i * unroll + u
                v = place_ref[b * block + n]
                where.append(lax.shift_right_logical(v, 10))
                kc = lax.bitwise_and(v, 1023)
                p = xbuf[slot, n]
                a = jnp.concatenate([p[:, :64], p[:, 64:]], axis=0)
                w = jnp.concatenate([w_ref[k, kc] for k in range(4)], axis=0)
                prod[u] = jnp.dot(a, w, preferred_element_type=jnp.float32)
            for u in range(unroll):
                acc[where[u]] += prod[u]
            return carry

        lax.fori_loop(0, block // unroll, group, 0)
        return carry

    lax.fori_loop(0, blocks, one_block, 0)
    if has_in:
        back.wait()
    if last:
        def finish(r, carry):
            held[r] = (acc[r] + before[r]).astype(held.dtype) if has_in else acc[r].astype(held.dtype)
            return carry

        lax.fori_loop(0, rows, finish, 0, unroll=4)
        away = pltpu.make_async_copy(held, out_hbm, sem.at[2])
    else:
        away = pltpu.make_async_copy(acc.at[pl.ds(0, rows)], out_hbm, sem.at[2])
    away.start()
    away.wait()


def products(place, x, parts, own, acc_in, row_local, last, block=128, unroll=32):
    has_in = acc_in is not None
    operands = (place, own, x, *parts) + ((acc_in,) if has_in else ())
    group, piece, rows, columns = parts[0].shape
    edge = rows * group
    result = jax.ShapeDtypeStruct((row_local, edge, columns), jnp.bfloat16 if last else jnp.float32)
    return pl.pallas_call(
        functools.partial(_product_kernel, has_in, last, block, unroll),
        in_specs=[pl.BlockSpec(memory_space=pltpu.SMEM)] * 2 + [pl.BlockSpec(memory_space=pl.ANY)] * (len(operands) - 2),
        out_specs=pl.BlockSpec(memory_space=pl.ANY),
        scratch_shapes=[
            pltpu.VMEM((row_local + 1, edge, columns), jnp.float32),
            pltpu.VMEM((4, 2 * group * piece, rows, columns), x.dtype),
            pltpu.VMEM((unroll, edge, columns), jnp.float32),
            pltpu.VMEM((2, block, 32, 128), x.dtype),
        ] + ([
            pltpu.VMEM((row_local, edge, columns), jnp.float32),
            pltpu.VMEM(result.shape, result.dtype),
        ] if has_in else []) + [
            pltpu.SemaphoreType.DMA((32,)),
            pltpu.SemaphoreType.DMA((2,)),
            pltpu.SemaphoreType.DMA((3,)),
        ],
        out_shape=result,
        compiler_params=pltpu.CompilerParams(vmem_limit_bytes=VMEM_LIMIT),
        name="products",
    )(*operands)


def shifted(value, axis):
    size = lax.axis_size(axis)
    return [lax.ppermute(value, axis, [(d, (d + s) % size) for d in range(size)]) for s in range(1, size)]


def look_up(coords, row_slot, kc_slot):
    count = row_slot.shape[0]
    lines = -(-count // 128)
    tables = jnp.pad(jnp.stack([row_slot, kc_slot]), ((0, 0), (0, lines * 128 - count)))
    tables = tables.reshape(2, lines, 128).astype(jnp.float32)
    line = (coords[:, :, None] // 128 == jnp.arange(lines)).astype(jnp.float32)
    picked = jnp.einsum(
        "tnh,thl->tnl", line, tables, precision=lax.Precision.HIGHEST, preferred_element_type=jnp.float32
    )
    lane = coords[:, :, None] % 128 == jnp.arange(128)
    found = jnp.sum(jnp.where(lane, picked, 0.0), axis=2).astype(jnp.int32)
    return found[0], found[1]


def body(amplitudes, tile_coords, row_slot, kc_slot, integrals):
    kc_groups = lax.axis_size("gz")
    planes = lax.axis_size("gx")
    devices = planes * lax.axis_size("zhi") * lax.axis_size("core") * kc_groups
    tile_count = amplitudes.shape[0]
    kc_piece, tile_edge, columns = integrals.shape
    row_local = 104
    gy_size = lax.axis_size("zhi") * lax.axis_size("core")
    part = tile_edge // planes
    quarter = lax.dynamic_slice_in_dim(integrals, lax.axis_index("gx") * part, part, 1)
    quarter = quarter.reshape(kc_piece * part, columns)
    pieces = [quarter] + shifted(quarter, "zhi")
    slab = jnp.concatenate(pieces, axis=0)

    row_pos, kc_pos = look_up(tile_coords.T, row_slot, kc_slot)
    kc_target = kc_pos // kc_piece % kc_groups
    kc_gy = kc_pos // (kc_groups * kc_piece)
    kc_row = kc_gy % 2 * (kc_piece * gy_size // 2) + kc_gy // 2 * kc_piece + kc_pos % kc_piece
    place = row_pos % row_local * 1024 + kc_row
    target = row_pos // row_local * kc_groups + kc_target
    ids = jnp.arange(tile_count, dtype=jnp.int32)
    same = (target[:, None] == target[None, :]) & (ids[None, :] < ids[:, None])
    rank = jnp.sum(same.astype(jnp.int32), axis=1)
    send_index = rank * devices + target
    send_ids = jnp.arange(devices * CAP, dtype=jnp.int32)
    matches = send_ids[:, None] == send_index[None, :]
    source = jnp.sum(jnp.where(matches, ids[None, :], 0), axis=1)
    empty = row_local * 1024
    sent_place = empty + jnp.sum(jnp.where(matches, place[None, :] - empty, 0), axis=1)
    source = source.reshape(CAP, devices)
    sent_place = sent_place.reshape(CAP, devices).T
    got_place = lax.all_to_all(sent_place, ALL, split_axis=0, concat_axis=0, tiled=True)

    acc = None
    start = 0
    relaid = None
    got = []
    for size in CHUNKS:
        src = source[start:start + size].T.reshape(-1)
        if relaid is None:
            sent, relaid = first_send(src, amplitudes, 64)
        else:
            sent, slab = next_send(src, relaid, slab, 64)
            across = [slab] + shifted(slab, "gx")
            swapped = [shifted(piece, "core")[0] for piece in across]
            across = across + held_until(swapped)
        arrived = lax.all_to_all(sent.reshape(devices, size * 32, 128), ALL, split_axis=0, concat_axis=0, tiled=True)
        got.append((arrived.reshape(devices * size, 32, 128), got_place[:, start:start + size].reshape(-1)))
        start += size
    own = jnp.stack([lax.axis_index(name) for name in ("gx", "zhi", "core")]).astype(jnp.int32)
    whole = [piece.reshape(-1, kc_piece, part, columns) for piece in across]
    for index, (tiles, places) in enumerate(got):
        acc = products(places, tiles, whole, own, acc, row_local, index == len(got) - 1)
    shared = lax.all_to_all(
        acc.reshape(kc_groups, row_local // kc_groups * tile_edge, columns), "gz", split_axis=0, concat_axis=0, tiled=True
    )
    total = jnp.sum(shared.astype(jnp.float32), axis=0).astype(jnp.bfloat16)
    total = total.reshape(row_local // kc_groups, 2, tile_edge // 2, columns)
    return jnp.swapaxes(total, 1, 2).reshape(row_local // kc_groups, tile_edge, columns)


def solution(mesh):
    gx, gy, gz = mesh.devices.shape
    fine = Mesh(mesh.devices.reshape(gx, gy // 2, 2, gz), ALL)
    placed = (
        P(ALL, None),
        P(ALL, None),
        P(),
        P(),
        P(GY + ("gz",), None, None),
    )

    return jax.shard_map(body, mesh=fine, in_specs=placed, out_specs=P(ALL, None, None), check_vma=False)
```

```python
import functools

import jax
import jax.numpy as jnp
from jax import lax
from jax.experimental import pallas as pl
from jax.experimental.pallas import tpu as pltpu
from jax.sharding import Mesh, PartitionSpec as P

ALL = ("gx", "zhi", "core", "gz")
GY = ("zhi", "core")
CAP = 4
RELAYOUT = 4
CHUNKS = (3, 1)
VMEM_LIMIT = 62 * 1024 * 1024


def _relayout_kernel(src_ref, place_ref, x_ref, out_ref, y_ref, *tmps):
    tiles = x_ref.shape[0]
    q_rows = x_ref.shape[1] // 128
    group = 8 * len(tmps)
    block, rows, _ = out_ref.shape
    taken = rows // q_rows
    devices = src_ref.shape[0] // taken
    base = pl.program_id(0) * block

    @pl.when(pl.program_id(0) == 0)
    def _():
        def one(g, carry):
            for t, tmp in enumerate(tmps):
                v = x_ref[pl.ds(pl.multiple_of(g * group, group) + 8 * t, 8), :].astype(jnp.float32)
                for q in range(q_rows):
                    tmp[pl.ds(q * 8, 8), :] = v[:, q * 128:(q + 1) * 128]
            for t, tmp in enumerate(tmps):
                for r in range(8):
                    y_ref[g * group + 8 * t + r] = tmp[pl.ds(r, q_rows, stride=8), :].astype(y_ref.dtype)
            return carry

        lax.fori_loop(0, tiles // group, one, 0)

    lane = lax.broadcasted_iota(jnp.int32, (8, 128), 1)
    slot = lane % CAP

    def send(g, carry):
        for u in range(8):
            d = g * 8 + u
            for k in range(taken):
                out_ref[d, pl.ds(k * q_rows, q_rows), :] = y_ref[src_ref[k * devices + base + d]]
            value = jnp.full((8, 128), place_ref[base + d], jnp.int32)
            for k in range(1, CAP):
                value = jnp.where(slot == k, place_ref[k * devices + base + d], value)
            high = lax.shift_right_logical(value, 10)
            middle = lax.bitwise_and(lax.shift_right_logical(value, 5), 31)
            low = lax.bitwise_and(value, 31)
            field = jnp.where(lane < CAP, high, jnp.where(lane < 2 * CAP, middle, low))
            out_ref[d, pl.ds(taken * q_rows, 8), :] = field.astype(jnp.float32).astype(out_ref.dtype)
        return carry

    lax.fori_loop(0, block // 8, send, 0)


def _copy_slots(src_ref, y_ref, out_ref):
    slots = out_ref.shape[0]
    base = pl.program_id(0) * slots

    def one(g, carry):
        for u in range(16):
            s = g * 16 + u
            out_ref[s] = y_ref[src_ref[base + s]]
        return carry

    lax.fori_loop(0, slots // 16, one, 0)


def _copy_kernel(src_ref, y_ref, held_ref, out_ref, kept_ref):
    _copy_slots(src_ref, y_ref, out_ref)


def first_send(src, place, x, taken, block):
    tiles, width = x.shape
    q_rows = width // 128
    devices = src.shape[0] // taken
    rows = taken * q_rows + 8
    return pl.pallas_call(
        _relayout_kernel,
        grid_spec=pltpu.PrefetchScalarGridSpec(
            num_scalar_prefetch=2,
            grid=(devices // block,),
            in_specs=[pl.BlockSpec((tiles, width), lambda i, s, p: (0, 0))],
            out_specs=[
                pl.BlockSpec((block, rows, 128), lambda i, s, p: (i, 0, 0)),
                pl.BlockSpec((tiles, q_rows, 128), lambda i, s, p: (0, 0, 0)),
            ],
            scratch_shapes=[pltpu.VMEM((8 * q_rows, 128), jnp.float32) for _ in range(RELAYOUT)],
        ),
        out_shape=[
            jax.ShapeDtypeStruct((devices, rows, 128), x.dtype),
            jax.ShapeDtypeStruct((tiles, q_rows, 128), x.dtype),
        ],
        compiler_params=pltpu.CompilerParams(vmem_limit_bytes=VMEM_LIMIT),
        name="first_send",
    )(src, place, x)


def next_send(src, y, held, block):
    slots = src.shape[0]
    return pl.pallas_call(
        _copy_kernel,
        grid_spec=pltpu.PrefetchScalarGridSpec(
            num_scalar_prefetch=1,
            grid=(slots // block,),
            in_specs=[
                pl.BlockSpec(y.shape, lambda i, s: (0, 0, 0)),
                pl.BlockSpec(memory_space=pl.ANY),
            ],
            out_specs=[
                pl.BlockSpec((block,) + y.shape[1:], lambda i, s: (i, 0, 0)),
                pl.BlockSpec(memory_space=pl.ANY),
            ],
        ),
        out_shape=[
            jax.ShapeDtypeStruct((slots,) + y.shape[1:], y.dtype),
            jax.ShapeDtypeStruct(held.shape, held.dtype),
        ],
        input_output_aliases={2: 1},
        compiler_params=pltpu.CompilerParams(vmem_limit_bytes=VMEM_LIMIT),
        name="next_send",
    )(src, y, held)


def _held_kernel(*refs):
    pass


def held_until(values):
    count = len(values)
    return list(pl.pallas_call(
        _held_kernel,
        in_specs=[pl.BlockSpec(memory_space=pl.ANY)] * count,
        out_specs=[pl.BlockSpec(memory_space=pl.ANY)] * count,
        out_shape=[jax.ShapeDtypeStruct(v.shape, v.dtype) for v in values],
        input_output_aliases={i: i for i in range(count)},
        name="held_until",
    )(*values))


def _product_kernel(has_in, last, block, unroll, start, taken, place_ref, own_ref, x_hbm, *rest):
    parts, rest = rest[:8], rest[8:]
    if has_in:
        acc_in, out_hbm, acc, w_ref, prod, xbuf, before, held, w_sem, x_sem, sem = rest
    else:
        out_hbm, acc, w_ref, prod, xbuf, w_sem, x_sem, sem = rest
    rows = out_hbm.shape[0]
    blocks = x_hbm.shape[0] // block

    def fetch(b, slot):
        return pltpu.make_async_copy(x_hbm.at[pl.ds(b * block, block)], xbuf.at[slot], x_sem.at[slot])

    copies = []
    for index, part in enumerate(parts):
        plane = lax.rem(own_ref[0] + 4 - index % 4, 4)
        core = lax.rem(own_ref[2] + index // 4, 2)
        for back_z in range(4):
            first = (core * 4 + lax.rem(own_ref[1] + 4 - back_z, 4)) * 50
            copies.append(pltpu.make_async_copy(
                part.at[back_z], w_ref.at[plane, pl.ds(first, 50)], w_sem.at[index * 4 + back_z]
            ))
    for copy in copies:
        copy.start()
    fetch(0, 0).start()
    if has_in:
        back = pltpu.make_async_copy(acc_in, before, sem.at[1])
        back.start()
    acc[...] = jnp.zeros_like(acc)
    for copy in copies:
        copy.wait()

    def one_block(b, carry):
        slot = lax.rem(b, 2)

        @pl.when(b + 1 < blocks)
        def _():
            fetch(b + 1, 1 - slot).start()

        fetch(b, slot).wait()

        def group(i, carry):
            where = []
            for t in range(unroll * taken):
                n, k = i * unroll + t // taken, t % taken
                v = place_ref[(b * block + n) * CAP + start + k]
                where.append(lax.shift_right_logical(v, 10))
                kc = lax.bitwise_and(v, 1023)
                p = xbuf[slot, n, pl.ds(k * 32, 32), :]
                a = jnp.concatenate([p[:, :64], p[:, 64:]], axis=0)
                w = jnp.concatenate([w_ref[q, kc] for q in range(4)], axis=0)
                prod[t] = jnp.dot(a, w, preferred_element_type=jnp.float32)
            for t in range(unroll * taken):
                acc[where[t]] += prod[t]
            return carry

        lax.fori_loop(0, block // unroll, group, 0)
        return carry

    lax.fori_loop(0, blocks, one_block, 0)
    if has_in:
        back.wait()
    if last:
        def finish(r, carry):
            held[r] = (acc[r] + before[r]).astype(held.dtype) if has_in else acc[r].astype(held.dtype)
            return carry

        lax.fori_loop(0, rows, finish, 0, unroll=4)
        away = pltpu.make_async_copy(held, out_hbm, sem.at[2])
    else:
        away = pltpu.make_async_copy(acc.at[pl.ds(0, rows)], out_hbm, sem.at[2])
    away.start()
    away.wait()


def products(place, x, parts, own, acc_in, row_local, last, start, taken, block, unroll):
    has_in = acc_in is not None
    operands = (place, own, x, *parts) + ((acc_in,) if has_in else ())
    group, piece, rows, columns = parts[0].shape
    edge = rows * group
    result = jax.ShapeDtypeStruct((row_local, edge, columns), jnp.bfloat16 if last else jnp.float32)
    return pl.pallas_call(
        functools.partial(_product_kernel, has_in, last, block, unroll, start, taken),
        in_specs=[pl.BlockSpec(memory_space=pltpu.SMEM)] * 2 + [pl.BlockSpec(memory_space=pl.ANY)] * (len(operands) - 2),
        out_specs=pl.BlockSpec(memory_space=pl.ANY),
        scratch_shapes=[
            pltpu.VMEM((row_local + 1, edge, columns), jnp.float32),
            pltpu.VMEM((4, 2 * group * piece, rows, columns), x.dtype),
            pltpu.VMEM((unroll * taken, edge, columns), jnp.float32),
            pltpu.VMEM((2, block) + x.shape[1:], x.dtype),
        ] + ([
            pltpu.VMEM((row_local, edge, columns), jnp.float32),
            pltpu.VMEM(result.shape, result.dtype),
        ] if has_in else []) + [
            pltpu.SemaphoreType.DMA((32,)),
            pltpu.SemaphoreType.DMA((2,)),
            pltpu.SemaphoreType.DMA((3,)),
        ],
        out_shape=result,
        compiler_params=pltpu.CompilerParams(vmem_limit_bytes=VMEM_LIMIT),
        name="products",
    )(*operands)


def shifted(value, axis):
    size = lax.axis_size(axis)
    return [lax.ppermute(value, axis, [(d, (d + s) % size) for d in range(size)]) for s in range(1, size)]


def look_up(coords, row_slot, kc_slot):
    count = row_slot.shape[0]
    lines = -(-count // 128)
    tables = jnp.pad(jnp.stack([row_slot, kc_slot]), ((0, 0), (0, lines * 128 - count)))
    tables = tables.reshape(2, lines, 128).astype(jnp.float32)
    line = (coords[:, :, None] // 128 == jnp.arange(lines)).astype(jnp.float32)
    picked = jnp.einsum(
        "tnh,thl->tnl", line, tables, precision=lax.Precision.HIGHEST, preferred_element_type=jnp.float32
    )
    lane = coords[:, :, None] % 128 == jnp.arange(128)
    found = jnp.sum(jnp.where(lane, picked, 0.0), axis=2).astype(jnp.int32)
    return found[0], found[1]


def body(amplitudes, tile_coords, row_slot, kc_slot, integrals):
    kc_groups = lax.axis_size("gz")
    planes = lax.axis_size("gx")
    devices = planes * lax.axis_size("zhi") * lax.axis_size("core") * kc_groups
    tile_count = amplitudes.shape[0]
    kc_piece, tile_edge, columns = integrals.shape
    row_local = 104
    gy_size = lax.axis_size("zhi") * lax.axis_size("core")
    part = tile_edge // planes
    quarter = lax.dynamic_slice_in_dim(integrals, lax.axis_index("gx") * part, part, 1)
    quarter = quarter.reshape(kc_piece * part, columns)
    pieces = [quarter] + shifted(quarter, "zhi")
    slab = jnp.concatenate(pieces, axis=0)

    row_pos, kc_pos = look_up(tile_coords.T, row_slot, kc_slot)
    kc_target = kc_pos // kc_piece % kc_groups
    kc_gy = kc_pos // (kc_groups * kc_piece)
    kc_row = kc_gy % 2 * (kc_piece * gy_size // 2) + kc_gy // 2 * kc_piece + kc_pos % kc_piece
    place = row_pos % row_local * 1024 + kc_row
    target = row_pos // row_local * kc_groups + kc_target
    ids = jnp.arange(tile_count, dtype=jnp.int32)
    same = (target[:, None] == target[None, :]) & (ids[None, :] < ids[:, None])
    rank = jnp.sum(same.astype(jnp.int32), axis=1)
    send_index = rank * devices + target
    send_ids = jnp.arange(devices * CAP, dtype=jnp.int32)
    matches = send_ids[:, None] == send_index[None, :]
    source = jnp.sum(jnp.where(matches, ids[None, :], 0), axis=1)
    empty = row_local * 1024
    sent_place = empty + jnp.sum(jnp.where(matches, place[None, :] - empty, 0), axis=1)
    source = source.reshape(CAP, devices)
    acc = None
    start = 0
    relaid = None
    got = []
    for size in CHUNKS:
        src = source[start:start + size].reshape(-1)
        if relaid is None:
            sent, relaid = first_send(src, sent_place, amplitudes, size, 32)
        else:
            sent, slab = next_send(src, relaid, slab, 64)
            across = [slab] + shifted(slab, "gx")
            swapped = [shifted(piece, "core")[0] for piece in across]
            across = across + held_until(swapped)
        arrived = lax.all_to_all(sent, ALL, split_axis=0, concat_axis=0, tiled=True)
        got.append((arrived, start, size))
        start += size
    fields = got[0][0][:, 32 * CHUNKS[0], :3 * CAP].astype(jnp.int32)
    places = (fields[:, :CAP] * 1024 + fields[:, CAP:2 * CAP] * 32 + fields[:, 2 * CAP:]).reshape(-1)
    own = jnp.stack([lax.axis_index(name) for name in ("gx", "zhi", "core")]).astype(jnp.int32)
    whole = [piece.reshape(-1, kc_piece, part, columns) for piece in across]
    for index, (tiles, start, size) in enumerate(got):
        last = index == len(got) - 1
        acc = products(
            places, tiles, whole, own, acc, row_local, last, start, size, 32 if size > 1 else 64, 8 if size > 1 else 32
        )
    shared = lax.all_to_all(
        acc.reshape(kc_groups, row_local // kc_groups * tile_edge, columns), "gz", split_axis=0, concat_axis=0, tiled=True
    )
    total = jnp.sum(shared.astype(jnp.float32), axis=0).astype(jnp.bfloat16)
    total = total.reshape(row_local // kc_groups, 2, tile_edge // 2, columns)
    return jnp.swapaxes(total, 1, 2).reshape(row_local // kc_groups, tile_edge, columns)


def solution(mesh):
    gx, gy, gz = mesh.devices.shape
    fine = Mesh(mesh.devices.reshape(gx, gy // 2, 2, gz), ALL)
    placed = (
        P(ALL, None),
        P(ALL, None),
        P(),
        P(),
        P(GY + ("gz",), None, None),
    )

    return jax.shard_map(body, mesh=fine, in_specs=placed, out_specs=P(ALL, None, None), check_vma=False)
```
